32 devices in a mesh: gx: 4 (over y, core), gy: 8 (over z, x).
Axes of the slice: x: 2, y: 2, z: 4, core: 2. Of those that a mesh axis runs over, the one named last changes fastest.
Arguments:
- motion_cotangent: float32 [3, 64, 128, 512], P(None, 'gx', 'gy'), may hold values from -8 to 8
- scaled_warmth: float32 [64, 128, 512], P('gx', 'gy'), may hold values from 0 to 1
- yielding_flags: int32 [64, 128, 512], P('gx', 'gy'), may hold values 0 or 1
- printed_flags: int32 [64, 128, 512], P('gx', 'gy'), may hold values 0 or 1
- material_label: int32 [64, 128, 512], P('gx', 'gy'), may hold values from 0 to 3
- phase_rigidity: float32 [4], replicated, may hold values from 0.5 to 4
- phase_dilatation: float32 [4], replicated, may hold values from 0.5 to 2
- phase_diffusivity: float32 [4], replicated, may hold values from 0.2 to 1
Outputs:
- adjoint_displacement: float32 [3, 64, 128, 512], P(None, 'gx', 'gy')
- thermal_adjoint: float32 [64, 128, 512], P('gx', 'gy')
The draws below stay inside these ranges and needn't reach their ends.
All inputs are finite; a program needn't handle non-finite values. No bound on the sum of `yielding_flags` or of `printed_flags` on one device may be relied on, other than what follows from the above.
Results may differ from the reference program's by a relative error of at most 0.0001.
Values sent between devices are 32-bit elements; how exact they have to be, the bound alone decides.
No kernel may reach another device: no remote copies, remote signals or barrier semaphores. Data moves between devices by JAX's collectives and lax.ppermute only.
A program may use at most 64 MiB of HBM per device.

```python
import math
import jax
import jax.numpy as jnp

POINTS_THIRD_DIM = 512
ITERS = 2
PHASES = 4
POINTS_FIRST_DIM = 64
POINTS_SECOND_DIM = 128


def draw_motion_cotangent(key, part):
    subkeys = jax.random.split(jax.random.fold_in(key, 17), 7)
    full_shape = (3, POINTS_FIRST_DIM, POINTS_SECOND_DIM, POINTS_THIRD_DIM)
    background = jax.random.normal(subkeys[0], full_shape, jnp.float32)
    shared_sign = jax.random.rademacher(subkeys[1], (3, 1, 1, 1), jnp.float32)
    shared_depth = jax.random.uniform(subkeys[2], (1, 1, 1, POINTS_THIRD_DIM), jnp.float32, 0.3, 0.6)
    row_signs = jax.random.rademacher(subkeys[3], (3, POINTS_FIRST_DIM, 1, 1), jnp.float32)
    column_signs = jax.random.rademacher(subkeys[4], (3, 1, POINTS_SECOND_DIM, 1), jnp.float32)
    depth_sign = jax.random.rademacher(subkeys[5], (3, 1, 1, POINTS_THIRD_DIM), jnp.float32)
    depth_size = jax.random.uniform(subkeys[6], (3, 1, 1, POINTS_THIRD_DIM), jnp.float32, 0.6, 1.0)
    layered = row_signs * column_signs * depth_sign * depth_size
    total = background + shared_sign * shared_depth + layered
    return jnp.clip(total, -8.0, 8.0).astype(jnp.float32)


def plant(array, key, low, top_value):
    place = [jax.random.randint(jax.random.fold_in(key, axis), (), 0, length) for axis, length in enumerate(array.shape)]
    main_axis = array.shape.index(max(array.shape))
    neighbour = place[:main_axis] + [(place[main_axis] + 1) % array.shape[main_axis]] + place[main_axis + 1:]
    return array.at[tuple(place)].set(low).at[tuple(neighbour)].set(top_value)


def block_scale(stream_key, extent, shards, low, largest):
    def one(axis_at, blocks):
        steps = jax.random.uniform(jax.random.fold_in(jax.random.fold_in(stream_key, 6), axis_at), (blocks,), jnp.float32, low / len(shards), largest / len(shards))
        return jnp.repeat(jnp.exp(steps), extent[axis_at] // blocks).reshape((-1,) + (1,) * (len(extent) - axis_at - 1))

    factor_of = one(*shards[0])
    for cut in shards[1:]:
        factor_of = factor_of * one(*cut)
    return factor_of


def setup_inputs(seed: int = 0) -> dict:
    arg_keys = jax.random.split(jax.random.key(seed), 9)
    motion_cotangent = draw_motion_cotangent(jax.random.fold_in(arg_keys[8], 71), 0)
    scaled_warmth = jnp.clip(1.0 * jax.random.uniform(arg_keys[1], (POINTS_FIRST_DIM, POINTS_SECOND_DIM, POINTS_THIRD_DIM), jnp.float32) ** block_scale(arg_keys[1], (POINTS_FIRST_DIM, POINTS_SECOND_DIM, POINTS_THIRD_DIM), ((0, 4), (1, 8)), -0.2, 0.2), 0.0, 1.0)
    yielding_flags = plant((jax.random.randint(arg_keys[2], (POINTS_FIRST_DIM, POINTS_SECOND_DIM, POINTS_THIRD_DIM), 0, 3) < 1).astype(jnp.int32), jax.random.fold_in(arg_keys[2], 1), 0, 1)
    printed_flags = plant((jax.random.randint(arg_keys[3], (POINTS_FIRST_DIM, POINTS_SECOND_DIM, POINTS_THIRD_DIM), 0, 4) < 3).astype(jnp.int32), jax.random.fold_in(arg_keys[3], 1), 0, 1)
    material_label = plant(jax.random.randint(arg_keys[4], (POINTS_FIRST_DIM, POINTS_SECOND_DIM, POINTS_THIRD_DIM), 0, PHASES), jax.random.fold_in(arg_keys[4], 1), 0, PHASES - 1).astype(jnp.int32)
    phase_rigidity = jnp.clip(jnp.exp(jax.random.uniform(arg_keys[5], (PHASES,), jnp.float32, math.log(0.5), math.log(4.0))), 0.5, 4.0)
    phase_dilatation = jnp.clip(jnp.exp(jax.random.uniform(arg_keys[6], (PHASES,), jnp.float32, math.log(0.5), math.log(2.0))), 0.5, 2.0)
    phase_diffusivity = jnp.clip(jnp.exp(jax.random.uniform(arg_keys[7], (PHASES,), jnp.float32, math.log(0.2), math.log(1.0))), 0.2, 1.0)
    return dict(motion_cotangent=motion_cotangent, scaled_warmth=scaled_warmth, yielding_flags=yielding_flags, printed_flags=printed_flags, material_label=material_label, phase_rigidity=phase_rigidity, phase_dilatation=phase_dilatation, phase_diffusivity=phase_diffusivity)


def pad_three(field):
    widths = [(0, 0)] * (field.ndim - 3) + [(1, 1)] * 3
    return jnp.pad(field, widths)


def neighbours(padded):
    return [padded[..., 2:, 1:-1, 1:-1], padded[..., :-2, 1:-1, 1:-1],
            padded[..., 1:-1, 2:, 1:-1], padded[..., 1:-1, :-2, 1:-1],
            padded[..., 1:-1, 1:-1, 2:], padded[..., 1:-1, 1:-1, :-2]]


def reference(motion_cotangent, scaled_warmth, yielding_flags, printed_flags, material_label, phase_rigidity, phase_dilatation, phase_diffusivity):
    hooke_tensor = jnp.take(phase_rigidity, material_label) * (1.0 - 0.7 * yielding_flags.astype(jnp.float32)) * (0.05 + 0.95 * printed_flags.astype(jnp.float32))
    conductance = jnp.take(phase_diffusivity, material_label)
    weights = [0.5 * (hooke_tensor + other) for other in neighbours(pad_three(hooke_tensor))]
    diagonal = 0.5 + sum(weights)

    def operate(field):
        beside_all = neighbours(pad_three(field))
        total = diagonal * field
        for weight, other in zip(weights, beside_all):
            total = total - weight * other
        return total

    solution = jnp.zeros_like(motion_cotangent)
    residual = motion_cotangent
    direction = motion_cotangent
    norm_now = jnp.sum(residual * residual)
    for iteration in range(ITERS):
        applied = operate(direction)
        step_size = norm_now / jnp.sum(direction * applied)
        solution = solution + step_size * direction
        residual = residual - step_size * applied
        norm_next = jnp.sum(residual * residual)
        direction = residual + (norm_next / norm_now) * direction
        norm_now = norm_next
    padded = pad_three(solution)
    flux_balance = padded[0, 2:, 1:-1, 1:-1] - padded[0, :-2, 1:-1, 1:-1]
    flux_balance = flux_balance + (padded[1, 1:-1, 2:, 1:-1] - padded[1, 1:-1, :-2, 1:-1])
    flux_balance = flux_balance + (padded[2, 1:-1, 1:-1, 2:] - padded[2, 1:-1, 1:-1, :-2])
    energy_input = -0.5 * jnp.take(phase_dilatation, material_label) * (0.5 + scaled_warmth) * hooke_tensor * flux_balance
    cond_near = neighbours(pad_three(conductance))
    source_near = neighbours(pad_three(energy_input))
    change = jnp.zeros_like(energy_input)
    for other_c, other_s in zip(cond_near, source_near):
        change = change + 0.5 * (conductance + other_c) * (other_s - energy_input)
    thermal = energy_input + 0.15 * change
    return solution, thermal
```

```python
import jax
import jax.numpy as jnp
from jax import lax
from jax.sharding import PartitionSpec as P

AXES = ("gx", "gy")


def exchange(array, axis, dim):
    count, length = lax.axis_size(axis), array.shape[dim]
    up = [(i, i + 1) for i in range(count - 1)]
    down = [(i + 1, i) for i in range(count - 1)]
    before = lax.ppermute(lax.slice_in_dim(array, length - 1, length, axis=dim), axis, up)
    after = lax.ppermute(lax.slice_in_dim(array, 0, 1, axis=dim), axis, down)
    return before, after


def shifted(array, halo, dim):
    before, after = halo
    length = array.shape[dim]
    inner_up = lax.slice_in_dim(array, 1, length, axis=dim)
    inner_down = lax.slice_in_dim(array, 0, length - 1, axis=dim)
    return (
        jnp.concatenate([inner_up, after], axis=dim),
        jnp.concatenate([before, inner_down], axis=dim),
    )


def depth_halo(array):
    zero = jnp.zeros_like(array[..., :1])
    return zero, zero


def six(array, x_halo, y_halo):
    ndim = array.ndim
    return (
        shifted(array, x_halo, ndim - 3)
        + shifted(array, y_halo, ndim - 2)
        + shifted(array, depth_halo(array), ndim - 1)
    )


def indexed_values(table, label):
    result = jnp.zeros(label.shape, jnp.float32)
    for index in range(table.shape[0]):
        result = result + jnp.where(label == index, table[index], 0.0)
    return result


def cut(halo, where):
    return tuple(part[where] for part in halo)


def per_device(motion, warmth, yielding, printed, label, rigidity, dilatation, diffusivity):
    stiffness = (
        indexed_values(rigidity, label)
        * (1.0 - 0.7 * yielding.astype(jnp.float32))
        * (0.05 + 0.95 * printed.astype(jnp.float32))
    )
    conductance = indexed_values(diffusivity, label)
    scaling = -0.5 * indexed_values(dilatation, label) * (0.5 + warmth) * stiffness
    first = jnp.concatenate([motion, stiffness[None], conductance[None]], axis=0)
    x_first, y_first = exchange(first, "gx", 1), exchange(first, "gy", 2)
    weights = [0.5 * (stiffness + o) for o in six(stiffness, cut(x_first, 3), cut(y_first, 3))]
    diagonal = 0.5 + sum(weights)
    links = [0.5 * (conductance + o) for o in six(conductance, cut(x_first, 4), cut(y_first, 4))]

    def operate(field, x_halo, y_halo):
        total = diagonal * field
        for weight, other in zip(weights, six(field, x_halo, y_halo)):
            total = total - weight * other
        return total

    three = slice(0, 3)
    x_motion, y_motion = cut(x_first, three), cut(y_first, three)
    q = operate(motion, x_motion, y_motion)
    x_q, y_q = exchange(q, "gx", 1), exchange(q, "gy", 2)
    z = operate(q, x_q, y_q)
    dot = lambda a, b: jnp.sum(a * b)
    rr, rq, qq, qz = dot(motion, motion), dot(motion, q), dot(q, q), dot(q, z)
    shift = jnp.where(qq > 0, rq / jnp.where(qq > 0, qq, 1.0), 0.0)
    u = motion - shift * q
    row = jnp.stack([rr, rq, qq, qz, shift, dot(u, u), dot(u, q), dot(u, z)])
    count = lax.axis_size(AXES)
    rows = lax.all_to_all(jnp.broadcast_to(row[None], (count, 8)), AXES, 0, 0)
    rr, rq, qq, qz, shift, uu, uq, uz = [rows[:, i] for i in range(8)]
    total_rr = jnp.sum(rr)
    step = total_rr / jnp.sum(rq)
    gap = step - shift
    next_rr = jnp.sum(uu - 2.0 * gap * uq + gap * gap * qq)
    energy = jnp.sum(
        (uq - shift * uz) - gap * (uz + qq - shift * qz) + gap * gap * qz
    )
    ratio = next_rr / total_rr
    next_step = next_rr / (energy - ratio * next_rr / step)
    c0 = step + next_step * (1.0 + ratio)
    c1 = -next_step * step
    solution = c0 * motion + c1 * q

    def divergence(field, x_halo, y_halo):
        x_up, x_down = shifted(field[0], cut(x_halo, 0), 0)
        y_up, y_down = shifted(field[1], cut(y_halo, 1), 1)
        z_up, z_down = shifted(field[2], depth_halo(field[2]), 2)
        return (x_up - x_down) + (y_up - y_down) + (z_up - z_down)

    sources = jnp.stack(
        [scaling * divergence(motion, x_motion, y_motion), scaling * divergence(q, x_q, y_q)]
    )
    x_s, y_s = exchange(sources, "gx", 1), exchange(sources, "gy", 2)
    mix = lambda pair: c0 * pair[0] + c1 * pair[1]
    source = mix(sources)
    change = jnp.zeros_like(source)
    near = six(source, tuple(map(mix, x_s)), tuple(map(mix, y_s)))
    for link, other in zip(links, near):
        change = change + link * (other - source)
    return solution, source + 0.15 * change


def solution(mesh):
    field = P("gx", "gy", None)
    in_specs = (P(None, "gx", "gy", None), field, field, field, field, P(), P(), P())
    out_specs = (P(None, "gx", "gy", None), field)
    return jax.shard_map(
        per_device, mesh=mesh, in_specs=in_specs, out_specs=out_specs, check_vma=False
    )
```

```python
import functools

import jax
import jax.numpy as jnp
from jax import lax
from jax.experimental import pallas as pl
from jax.experimental.pallas import tpu as pltpu
from jax.sharding import PartitionSpec as P

AXES = ("gx", "gy")
INTERPRET = False
F32 = jnp.float32
VMEM = pl.BlockSpec(memory_space=pltpu.VMEM)
SMEM = pl.BlockSpec(memory_space=pltpu.SMEM)

SIDE = 10
CORNER_ROWS = 24


def call(kernel, out_shape, in_specs, out_specs=None, **extra):
    out_specs = jax.tree.map(lambda _: VMEM, out_shape) if out_specs is None else out_specs
    return pl.pallas_call(
        kernel, out_shape=out_shape, in_specs=in_specs, out_specs=out_specs, interpret=INTERPRET, **extra
    )


def shape(*dims):
    return jax.ShapeDtypeStruct(dims, F32)


def z_pair(value):
    length = value.shape[-1]
    lane = lax.broadcasted_iota(jnp.int32, value.shape, value.ndim - 1)
    after = jnp.where(lane == length - 1, 0.0, pltpu.roll(value, length - 1, value.ndim - 1))
    before = jnp.where(lane == 0, 0.0, pltpu.roll(value, 1, value.ndim - 1))
    return after, before


def row_pair(value, row_before, row_after):
    length = value.shape[0]
    row = lax.broadcasted_iota(jnp.int32, value.shape, 0)
    after = jnp.where(row == length - 1, row_after, pltpu.roll(value, length - 1, 0))
    before = jnp.where(row == 0, row_before, pltpu.roll(value, 1, 0))
    return after, before


def apply(center, lead_before, lead_after, row_before, row_after):
    near = [
        (a, b) + row_pair(c, p, n) + z_pair(c)
        for c, b, a, p, n in zip(center, lead_before, lead_after, row_before, row_after)
    ]
    weights = [center[0] + other for other in near[0]]
    diagonal = 0.5 + sum(weights)
    out = []
    for value, others in zip(center[1:], near[1:]):
        total = diagonal * value
        for weight, other in zip(weights, others):
            total = total - weight * other
        out.append(total)
    return out


def lookup(label, table):
    count = table.shape[0]
    value = jnp.full(label.shape, table[count - 1], F32)
    for index in range(count - 1):
        value = jnp.where(label == index, table[index], value)
    return value


def prepare_kernel(
    rigidity, dilatation, diffusivity, motion, warmth, yielding, printed, label,
    half, kappa, links, y_down, y_up, late_down, late_up, x_down, x_up,
):
    depth_x, rows = half.shape[0], half.shape[1]
    for x in range(depth_x):
        kind = label[x]
        h = (
            0.5 * lookup(kind, rigidity)
            * (1.0 - 0.7 * yielding[x].astype(F32))
            * (0.05 + 0.95 * printed[x].astype(F32))
        )
        half[x] = h
        kappa[x] = -lookup(kind, dilatation) * (0.5 + warmth[x]) * h
        links[x] = 0.075 * lookup(kind, diffusivity)
    for x in range(depth_x):
        for out, late, order in ((y_down, late_down, (0, 1, 2)), (y_up, late_up, (rows - 1, rows - 2, rows - 3))):
            for depth in range(2):
                at = pl.ds(order[depth], 1)
                for c in range(3):
                    out[4 * depth + c, pl.ds(x, 1), :] = motion[c, x, at, :]
                out[4 * depth + 3, pl.ds(x, 1), :] = half[x, at, :]
            late[0, pl.ds(x, 1), :] = motion[1, x, pl.ds(order[2], 1), :]
            late[1, pl.ds(x, 1), :] = half[x, pl.ds(order[2], 1), :]
            late[2, pl.ds(x, 1), :] = kappa[x, pl.ds(order[0], 1), :]
            late[3, pl.ds(x, 1), :] = links[x, pl.ds(order[0], 1), :]

    def planes(out, order):
        for depth in range(2):
            for c in range(3):
                out[4 * depth + c] = motion[c, order[depth]]
            out[4 * depth + 3] = half[order[depth]]
        out[8] = motion[0, order[2]]
        out[9] = half[order[2]]
        out[10] = kappa[order[0]]
        out[11] = links[order[0]]

    @pl.when(pl.program_id(0) == 0)
    def _():
        planes(x_down, (0, 1, 2))

    @pl.when(pl.program_id(0) == pl.num_programs(0) - 1)
    def _():
        planes(x_up, (depth_x - 1, depth_x - 2, depth_x - 3))


def prepare(motion, warmth, yielding, printed, label, rigidity, dilatation, diffusivity):
    _, nx, ny, nz = motion.shape
    block = 8
    field = pl.BlockSpec((block, ny, nz), lambda i: (i, 0, 0))
    rows = lambda n: pl.BlockSpec((n, block, nz), lambda i: (0, i, 0))
    whole = pl.BlockSpec((12, ny, nz), lambda i: (0, 0, 0))
    return call(
        prepare_kernel,
        (shape(nx, ny, nz),) * 3
        + (shape(8, nx, nz),) * 2 + (shape(4, nx, nz),) * 2 + (shape(12, ny, nz),) * 2,
        [SMEM] * 3 + [pl.BlockSpec((3, block, ny, nz), lambda i: (0, i, 0, 0))] + [field] * 4,
        (field,) * 3 + (rows(8),) * 2 + (rows(4),) * 2 + (whole,) * 2,
        grid=(nx // block,),
    )(rigidity, dilatation, diffusivity, motion, warmth, yielding, printed, label)


def corner_kernel(x_low, x_high, down, up):
    rows = x_low.shape[1]
    for side, planes in ((0, x_low), (SIDE, x_high)):
        for out, near, far in ((down, 0, 1), (up, rows - 1, rows - 2)):
            for k, plane in enumerate((0, 1, 2, 3, 4, 5, 7)):
                out[pl.ds(side + k, 1), :] = planes[plane, pl.ds(near, 1), :]
            for k, plane in enumerate((0, 1, 3)):
                out[pl.ds(side + 7 + k, 1), :] = planes[plane, pl.ds(far, 1), :]
    for out in (down, up):
        out[pl.ds(2 * SIDE, CORNER_ROWS - 2 * SIDE), :] = jnp.zeros((CORNER_ROWS - 2 * SIDE, out.shape[1]), F32)


def corners(x_low, x_high):
    _, ny, nz = x_low.shape
    return call(
        corner_kernel, (shape(CORNER_ROWS, nz),) * 2,
        [pl.BlockSpec((8, ny, nz), lambda i: (0, 0, 0))] * 2,
        (pl.BlockSpec((CORNER_ROWS, nz), lambda i: (0, 0)),) * 2, grid=(1,),
    )(x_low, x_high)


def fold(value):
    rows, length = value.shape
    value = sum(value[8 * k : 8 * k + 8] for k in range(rows // 8))
    return sum(value[:, 128 * k : 128 * k + 128] for k in range(length // 128))


def total(value):
    return jnp.sum(jnp.sum(value, axis=1, keepdims=True), axis=0, keepdims=True)


def over(planes, body, carry):
    carry = body(0, True, False, carry)
    carry = lax.fori_loop(1, planes - 1, lambda x, c: body(x, False, False, c), carry)
    return body(planes - 1, False, True, carry)


def sums_kernel(
    motion, half, x_low, x_high, y_low, y_high, c_low, c_high, own_low, own_high, q, qx, qy, rows_out
):
    nx, ny, nz = half.shape
    row = lambda ref, k: ref[pl.ds(k, 1), :]
    planes = lambda ref, base: [ref[base + 3], ref[base], ref[base + 1], ref[base + 2]]
    lines = lambda ref, base: [row(ref, base + k) for k in (3, 0, 1, 2)]
    own = lambda x: [half[x], motion[0, x], motion[1, x], motion[2, x]]
    beyond = lambda ref, x: [ref[k, pl.ds(x, 1), :] for k in (3, 0, 1, 2)]

    def store(out, base, center, values):
        for c, value in enumerate(values):
            out[base + c] = jnp.where(center[0] > 0.0, value, 0.0)

    near = planes(x_low, 0)
    store(qx, 0, near, apply(near, planes(x_low, 4), own(0), lines(c_low, 0), lines(c_high, 0)))
    near = planes(x_high, 0)
    store(qx, 3, near, apply(near, own(nx - 1), planes(x_high, 4), lines(c_low, SIDE), lines(c_high, SIDE)))
    near = planes(y_low, 0)
    store(qy, 0, near, apply(near, planes(y_low, 4), planes(own_low, 0), lines(c_low, 0), lines(c_low, SIDE)))
    near = planes(y_high, 0)
    store(qy, 3, near, apply(near, planes(own_high, 0), planes(y_high, 4), lines(c_high, 0), lines(c_high, SIDE)))

    def first(x, is_first, is_last, carry):
        rr, rq, qq = carry
        center = own(x)
        before = planes(x_low, 0) if is_first else own(x - 1)
        after = planes(x_high, 0) if is_last else own(x + 1)
        values = apply(center, before, after, beyond(y_low, x), beyond(y_high, x))
        for c, (r, value) in enumerate(zip(center[1:], values)):
            q[c, x] = value
            rr, rq, qq = rr + fold(r * r), rq + fold(r * value), qq + fold(value * value)
        return rr, rq, qq

    zero = jnp.zeros((8, 128), F32)
    rr, rq, qq = map(total, over(nx, first, (zero,) * 3))
    shift = jnp.where(qq > 0.0, rq / jnp.where(qq > 0.0, qq, 1.0), 0.0)

    def second(x, is_first, is_last, carry):
        uu, uq, uz, qz = carry
        values = lambda ref, at: [ref[at(c)] for c in range(3)]
        center = [half[x]] + [q[c, x] for c in range(3)]
        before = [x_low[3]] + [qx[c] for c in range(3)] if is_first else [half[x - 1]] + [q[c, x - 1] for c in range(3)]
        after = [x_high[3]] + [qx[3 + c] for c in range(3)] if is_last else [half[x + 1]] + [q[c, x + 1] for c in range(3)]
        low = [y_low[3, pl.ds(x, 1), :]] + [qy[c, pl.ds(x, 1), :] for c in range(3)]
        high = [y_high[3, pl.ds(x, 1), :]] + [qy[3 + c, pl.ds(x, 1), :] for c in range(3)]
        for c, z in enumerate(apply(center, before, after, low, high)):
            u = motion[c, x] - shift * center[1 + c]
            uu, uq = uu + fold(u * u), uq + fold(u * center[1 + c])
            uz, qz = uz + fold(u * z), qz + fold(center[1 + c] * z)
        return uu, uq, uz, qz

    uu, uq, uz, qz = map(total, over(nx, second, (zero,) * 4))
    lane = lax.broadcasted_iota(jnp.int32, (1, 128), 1)
    line = jnp.zeros((1, 128), F32)
    for k, value in enumerate((rr, rq, qq, qz, shift, uu, uq, uz)):
        line = jnp.where(lane == k, value, line)
    rows_out[...] = jnp.broadcast_to(line, rows_out.shape)


def late_kernel(
    x_low, x_high, y_low, y_high, late_low, late_high, c_low, c_high, q_x, q_y, q_corner,
):
    row = lambda ref, k: ref[pl.ds(k, 1), :]
    masked = lambda h, value: jnp.where(h > 0.0, value, 0.0)
    ny, nx = x_low.shape[1], y_low.shape[1]

    def one(center, before, after, low, high):
        return masked(center[0], apply(center, before, after, low, high)[0])

    p = lambda ref, *ks: [ref[k] for k in ks]
    r = lambda ref, *ks: [row(ref, k) for k in ks]
    q_x[0] = one(p(x_low, 7, 4), p(x_low, 9, 8), p(x_low, 3, 0), r(c_low, 6, 4), r(c_high, 6, 4))
    q_x[1] = one(p(x_high, 7, 4), p(x_high, 3, 0), p(x_high, 9, 8), r(c_low, SIDE + 6, SIDE + 4), r(c_high, SIDE + 6, SIDE + 4))
    q_y[0] = one(p(y_low, 7, 5), p(late_low, 1, 0), p(y_low, 3, 1), r(c_low, 9, 8), r(c_low, SIDE + 9, SIDE + 8))
    q_y[1] = one(p(y_high, 7, 5), p(y_high, 3, 1), p(late_high, 1, 0), r(c_high, 9, 8), r(c_high, SIDE + 9, SIDE + 8))
    q_corner[...] = jnp.zeros(q_corner.shape, F32)
    for k, (c, base, x, y, px, py) in enumerate((
        (c_low, 0, 0, 0, x_low, y_low),
        (c_low, SIDE, nx - 1, 0, x_high, y_low),
        (c_high, 0, 0, ny - 1, x_low, y_high),
        (c_high, SIDE, nx - 1, ny - 1, x_high, y_high),
    )):
        h = row(c, base + 3)
        beside = lambda plane, out_x, out_y: [
            row(c, base + out_x), row(c, base + out_y), py[plane, pl.ds(x, 1), :], px[plane, pl.ds(y, 1), :]
        ]
        h_near = beside(3, 6, 9)
        for comp in range(2):
            value = row(c, base + comp)
            acc = 0.5 * value
            for hn, vn in zip(h_near + list(z_pair(h)), beside(comp, 4 + comp, 7 + comp) + list(z_pair(value))):
                acc = acc + (h + hn) * (value - vn)
            q_corner[pl.ds(4 * comp + k, 1), :] = masked(h, acc)


def finish_kernel(
    rows, motion, q, kappa, links, x_low, x_high, y_low, y_high, late_low, late_high, c_low, c_high,
    qx, qy, q_x, q_y, q_corner, solution, thermal, source, source_low, source_high, edge,
):
    nx, ny, nz = kappa.shape
    table = rows[...]
    column = lambda k: table[:, k : k + 1]
    summed = lambda value: jnp.sum(value, axis=0, keepdims=True)
    rr, rq, qq, qz, shift, uu, uq, uz = [column(k) for k in range(8)]
    total_rr = summed(rr)
    step = total_rr / summed(rq)
    gap = step - shift
    next_rr = summed(uu - 2.0 * gap * uq + gap * gap * qq)
    energy = summed((uq - shift * uz) - gap * (uz + qq - shift * qz) + gap * gap * qz)
    ratio = next_rr / total_rr
    next_step = next_rr / (energy - ratio * next_rr / step)
    c0 = step + next_step * (1.0 + ratio)
    c1 = -next_step * step
    mix = lambda a, b: c0 * a + c1 * b
    row = lambda ref, k: ref[pl.ds(k, 1), :]

    def z_diff(value):
        after, before = z_pair(value)
        return after - before

    def row_diff(value, row_before, row_after):
        after, before = row_pair(value, row_before, row_after)
        return after - before

    def combine(x, carry):
        for c in range(3):
            solution[c, x] = mix(motion[c, x], q[c, x])
        edge[0, pl.ds(x, 1), :] = solution[1, x, pl.ds(0, 1), :]
        edge[1, pl.ds(x, 1), :] = solution[1, x, pl.ds(ny - 1, 1), :]
        return carry

    for x in range(nx):
        combine(x, 0)
    corner = lambda c_ref, base, comp, k: mix(row(c_ref, base + comp), row(q_corner, 4 * comp + k))
    x_of = lambda planes, base, c: mix(planes[c], qx[base + c])
    y_of = lambda planes, base, c: mix(planes[c], qy[base + c])
    s_x_low = x_low[10] * (
        solution[0, 0] - mix(x_low[4], q_x[0])
        + row_diff(x_of(x_low, 0, 1), corner(c_low, 0, 1, 0), corner(c_high, 0, 1, 2))
        + z_diff(x_of(x_low, 0, 2))
    )
    s_x_high = x_high[10] * (
        mix(x_high[4], q_x[1]) - solution[0, nx - 1]
        + row_diff(x_of(x_high, 3, 1), corner(c_low, SIDE, 1, 1), corner(c_high, SIDE, 1, 3))
        + z_diff(x_of(x_high, 3, 2))
    )
    source_low[...] = late_low[2] * (
        row_diff(y_of(y_low, 0, 0), corner(c_low, 0, 0, 0), corner(c_low, SIDE, 0, 1))
        + edge[0] - mix(y_low[5], q_y[0]) + z_diff(y_of(y_low, 0, 2))
    )
    source_high[...] = late_high[2] * (
        row_diff(y_of(y_high, 3, 0), corner(c_high, 0, 0, 2), corner(c_high, SIDE, 0, 3))
        + mix(y_high[5], q_y[1]) - edge[1] + z_diff(y_of(y_high, 3, 2))
    )

    def first(x, is_first, is_last, carry):
        before = x_of(x_low, 0, 0) if is_first else solution[0, x - 1]
        after = x_of(x_high, 3, 0) if is_last else solution[0, x + 1]
        low = mix(y_low[1, pl.ds(x, 1), :], qy[1, pl.ds(x, 1), :])
        high = mix(y_high[1, pl.ds(x, 1), :], qy[4, pl.ds(x, 1), :])
        source[x] = kappa[x] * (after - before + row_diff(solution[1, x], low, high) + z_diff(solution[2, x]))
        return carry

    over(nx, first, 0)

    def second(x, is_first, is_last, carry):
        s, g = source[x], links[x]
        s_before, g_before = (s_x_low, x_low[11]) if is_first else (source[x - 1], links[x - 1])
        s_after, g_after = (s_x_high, x_high[11]) if is_last else (source[x + 1], links[x + 1])
        at = pl.ds(x, 1)
        s_near = (s_before, s_after) + row_pair(s, source_low[at, :], source_high[at, :]) + z_pair(s)
        g_near = (g_before, g_after) + row_pair(g, late_low[3, at, :], late_high[3, at, :]) + z_pair(g)
        value = s
        for sn, gn in zip(s_near, g_near):
            value = value + (g + gn) * (sn - s)
        thermal[x] = value
        return carry

    over(nx, second, 0)


def per_device(motion, warmth, yielding, printed, label, rigidity, dilatation, diffusivity):
    _, nx, ny, nz = motion.shape
    devices = lax.axis_size(AXES)

    def swap(axis, down, up):
        count = lax.axis_size(axis)
        high = lax.ppermute(down, axis, [(i + 1, i) for i in range(count - 1)])
        low = lax.ppermute(up, axis, [(i, i + 1) for i in range(count - 1)])
        return low, high

    half, kappa, links, y_down, y_up, late_down, late_up, x_down, x_up = prepare(
        motion, warmth, yielding, printed, label, rigidity, dilatation, diffusivity
    )
    x_low, x_high = swap("gx", x_down, x_up)
    y_low, y_high = swap("gy", y_down, y_up)
    c_low, c_high = swap("gy", *corners(x_low, x_high))
    late_low, late_high = swap("gy", late_down, late_up)
    q, qx, qy, rows = call(
        sums_kernel,
        (shape(3, nx, ny, nz), shape(6, ny, nz), shape(6, nx, nz), shape(devices, 128)),
        [VMEM] * 10,
    )(motion, half, x_low, x_high, y_low, y_high, c_low, c_high, y_down, y_up)
    rows = lax.all_to_all(rows, AXES, 0, 0, tiled=True)
    q_x, q_y, q_corner = call(
        late_kernel, (shape(2, ny, nz), shape(2, nx, nz), shape(8, nz)), [VMEM] * 8
    )(x_low, x_high, y_low, y_high, late_low, late_high, c_low, c_high)
    return call(
        finish_kernel,
        (shape(3, nx, ny, nz), shape(nx, ny, nz)),
        [VMEM] * 18,
        scratch_shapes=[
            pltpu.VMEM((nx, ny, nz), F32), pltpu.VMEM((nx, nz), F32),
            pltpu.VMEM((nx, nz), F32), pltpu.VMEM((2, nx, nz), F32),
        ],
    )(
        rows, motion, q, kappa, links, x_low, x_high, y_low, y_high, late_low, late_high, c_low, c_high,
        qx, qy, q_x, q_y, q_corner,
    )


def solution(mesh):
    field = P("gx", "gy", None)
    in_specs = (P(None, "gx", "gy", None), field, field, field, field, P(), P(), P())
    out_specs = (P(None, "gx", "gy", None), field)
    return jax.shard_map(
        per_device, mesh=mesh, in_specs=in_specs, out_specs=out_specs, check_vma=False
    )
```
